32 devices in a mesh: dp: 16 (over z, y, core), inner: 2 (over x).
Axes of the slice: x: 2, y: 2, z: 4, core: 2. Of those that a mesh axis runs over, the one named last changes fastest.
Arguments:
- inputs: bfloat16 [32, 32, 32, 256], P(('dp', 'inner')), may hold values from -24 to 24
- cotangent: bfloat16 [32, 32, 32, 256], P(('dp', 'inner')), may hold values from -24 to 24
- kernel_taps: float32 [9, 256, 256], P(None, 'dp', 'inner'), may hold values from -1 to 1
Outputs:
- new_taps: float32 [9, 256, 256], P(None, 'dp', 'inner')
The draws below stay inside these ranges and needn't reach their ends.
All inputs are finite; a program needn't handle non-finite values.
Results may differ from the reference program's by a relative error of at most 0.0003.
Values sent between devices are 32-bit elements; how exact they have to be, the bound alone decides.
No kernel may reach another device: no remote copies, remote signals or barrier semaphores. Data moves between devices by JAX's collectives and lax.ppermute only.
A program may use at most 64 MiB of HBM per device.

```python
import math
import jax
import jax.numpy as jnp
from jax import lax

CHANNELS = 256
MAPSIDE = 32
BATCH = 32
FREQS = 544
N_DP = 16
N_INNER = 2


def scaled_field(key, salt):
    field_key, scale_key = jax.random.split(jax.random.fold_in(key, salt))
    shape = (BATCH, MAPSIDE, MAPSIDE, CHANNELS)
    position = jnp.arange(CHANNELS, dtype=jnp.float32) / CHANNELS
    rough = jax.random.uniform(scale_key, (CHANNELS,), jnp.float32, 0.8, 1.25)
    values = jnp.clip(jax.random.normal(field_key, shape, jnp.float32), -6.0, 6.0)
    scales = jnp.power(2.0, position) * rough
    return (values * scales).astype(jnp.bfloat16)


def draw_inputs(key, part):
    return scaled_field(key, 17)


def draw_cotangent(key, part):
    return scaled_field(key, 29)


def draw_kernel_taps(key, part):
    shape = (9, CHANNELS, CHANNELS)
    tap_key = jax.random.fold_in(key, 41)
    tap_scale = jnp.where(jnp.arange(9) == 4, 0.6, 0.3 / math.sqrt(8.0)) / math.sqrt(CHANNELS)
    values = jnp.clip(jax.random.normal(tap_key, shape, jnp.float32), -4.0, 4.0)
    return (values * tap_scale[:, None, None]).astype(jnp.float32)


def setup_inputs(seed: int = 0) -> dict:
    keys = jax.random.split(jax.random.key(seed), 4)
    return {
        "inputs": draw_inputs(jax.random.fold_in(keys[3], 71), 0),
        "cotangent": draw_cotangent(jax.random.fold_in(keys[3], 71), 0),
        "kernel_taps": draw_kernel_taps(jax.random.fold_in(keys[3], 71), 0),
    }


step_share = 0.06

def matmul(left_side, right_side):
    return jnp.dot(left_side, right_side, precision=lax.Precision.HIGHEST, preferred_element_type=jnp.float32)

def gradient_terms(inputs, cotangent):
    channels = inputs.shape[3]
    flat_cotangent = cotangent.reshape(-1, channels)
    collected = []
    for tap_index in range(9):
        row_off = tap_index // 3 - 1
        col_off = tap_index % 3 - 1
        shifted = jnp.roll(inputs, (-row_off, -col_off), axis=(1, 2))
        collected.append(lax.dot_general(shifted.reshape(-1, channels), flat_cotangent, (((0,), (0,)), ((), ())), preferred_element_type=jnp.float32))
    return jnp.stack(collected)

def phase_tables(freq_index, mapside, freq_count):
    row_shift = jnp.array([-1, -1, -1, 0, 0, 0, 1, 1, 1], dtype=jnp.int32)
    col_shift = jnp.array([-1, 0, 1, -1, 0, 1, -1, 0, 1], dtype=jnp.int32)
    half_width = mapside // 2 + 1
    first_freq = freq_index // half_width
    second_freq = freq_index % half_width
    turn_count = (first_freq[:, None] * row_shift[None, :] + second_freq[:, None] * col_shift[None, :]) % mapside
    phase_angle = turn_count.astype(jnp.float32) * (2.0 * math.pi / mapside)
    live_mask = (freq_index < freq_count).astype(jnp.float32)[:, None]
    return (jnp.cos(phase_angle) * live_mask, jnp.sin(phase_angle) * live_mask)

def inverse_tables(freq_index, mapside, freq_count):
    cos_table, sin_table = phase_tables(freq_index, mapside, freq_count)
    second_freq = freq_index % (mapside // 2 + 1)
    on_edge = (second_freq == 0) | (second_freq == mapside // 2)
    weight = jnp.where(on_edge, 1.0, 2.0).astype(jnp.float32) / (mapside * mapside)
    return (cos_table * weight[:, None], sin_table * weight[:, None])

def bjorck(real_part, imag_part):
    matrix_size = real_part.shape[0]
    identity = jnp.eye(matrix_size, dtype=jnp.float32)
    for iteration in range(2):
        products = matmul(real_part.T, jnp.concatenate([real_part, imag_part], axis=1))
        square = matmul(imag_part.T, imag_part)
        cross_part = products[:, matrix_size:]
        gram_real = products[:, :matrix_size] + square
        gram_imag = cross_part - cross_part.T
        mix_real = 1.5 * identity - 0.5 * gram_real
        mix_imag = -0.5 * gram_imag
        stacked = jnp.concatenate([jnp.concatenate([mix_real, mix_imag], axis=1), jnp.concatenate([-mix_imag, mix_real], axis=1)], axis=0)
        joined = matmul(jnp.concatenate([real_part, imag_part], axis=1), stacked)
        real_part, imag_part = (joined[:, :matrix_size], joined[:, matrix_size:])
    return (real_part, imag_part)

def reference(inputs, cotangent, kernel_taps):
    channels = CHANNELS
    input_blocks = inputs.reshape(N_DP * N_INNER, -1, MAPSIDE, MAPSIDE, channels)
    cotan_blocks = cotangent.reshape(N_DP * N_INNER, -1, MAPSIDE, MAPSIDE, channels)

    def accumulate(carried, matrices):
        return (carried + gradient_terms(matrices[0], matrices[1]), None)
    gradient, _ = lax.scan(accumulate, jnp.zeros((9, channels, channels), jnp.float32), (input_blocks, cotan_blocks))
    grad_norm = jnp.sqrt(jnp.sum(gradient * gradient))
    step_factor = step_share * math.sqrt(channels) / (grad_norm + 1e-06)
    updated = kernel_taps - step_factor * gradient
    flattened = updated.reshape(9, channels * channels)

    def per_freq(carried, freq_index):
        index_row = freq_index[None]
        cos_table, sin_table = phase_tables(index_row, MAPSIDE, FREQS)
        real_part = matmul(cos_table, flattened).reshape(channels, channels)
        imag_part = -matmul(sin_table, flattened).reshape(channels, channels)
        real_part, imag_part = bjorck(real_part, imag_part)
        weighted_cos, weighted_sin = inverse_tables(index_row, MAPSIDE, FREQS)
        contribution = matmul(weighted_cos.T, real_part.reshape(1, -1)) - matmul(weighted_sin.T, imag_part.reshape(1, -1))
        return (carried + contribution, None)
    rebuilt, _ = lax.scan(per_freq, jnp.zeros((9, channels * channels), jnp.float32), jnp.arange(FREQS, dtype=jnp.int32))
    return (math.sqrt(channels) * rebuilt).reshape(9, channels, channels)
```

```python
import functools
import math

import jax
import jax.numpy as jnp
import numpy as np
from jax import lax
from jax.experimental import pallas as pl
from jax.experimental.pallas import tpu as pltpu
from jax.sharding import PartitionSpec as P

F32 = jnp.float32
BF16 = jnp.bfloat16

step_share = 0.06


def split(value):
    high = value.astype(BF16)
    return high, (value - high.astype(F32)).astype(BF16)


def mm(left, right, contract=(1, 0)):
    dims = (((contract[0],), (contract[1],)), ((), ()))
    return lax.dot_general(left, right, dims, preferred_element_type=F32)


def mm3(left, right, contract=(1, 0)):
    (lh, ll), (rh, rl) = left, right
    return mm(lh, rh, contract) + (mm(lh, rl, contract) + mm(ll, rh, contract))


def total(terms):
    return functools.reduce(lambda a, b: a + b, terms)


def hermitian_square(held):
    skew = 0.5 * (held - held.T)
    held_parts, skew_parts = split(held), split(skew)
    return mm3(held_parts, held_parts) - 2.0 * mm3(skew_parts, skew_parts)


def ortho_kernel(trip_count, row_ref, unit_ref, taps_ref, out_ref, base_ref, acc_ref, vr_ref, vi_ref):
    size = taps_ref.shape[1]
    cos_row, sin_row = row_ref[0], row_ref[1]
    diag = lax.broadcasted_iota(jnp.int32, (size, size), 0) == lax.broadcasted_iota(jnp.int32, (size, size), 1)
    for b in range(3):
        vr_ref[b] = taps_ref[3 + b] + cos_row * (taps_ref[6 + b] + taps_ref[b])
        vi_ref[b] = -sin_row * (taps_ref[6 + b] - taps_ref[b])
    own = []
    for b in range(3):
        x, y = vr_ref[b], vi_ref[b]
        y_parts = split(y)
        own.append(mm3(split(x - y), split(x + y), (0, 0)) + 2.0 * mm3(y_parts, y_parts, (0, 0)))
    base_ref[0] = jnp.where(diag, 1.5, 0.0) - 0.5 * total(own)
    for slot, pairs in ((1, ((1, 0), (2, 1))), (3, ((2, 0),))):
        plus, minus = [], []
        for left, right in pairs:
            ar, ai = split(vr_ref[left]), split(vi_ref[left])
            add = split(vr_ref[right] + vi_ref[right])
            sub = split(vr_ref[right] - vi_ref[right])
            plus.append(mm3(ar, add, (0, 0)) - mm3(ai, sub, (0, 0)))
            minus.append(mm3(ar, sub, (0, 0)) + mm3(ai, add, (0, 0)))
        plus, minus = total(plus), total(minus)
        base_ref[slot] = -0.5 * (plus + minus.T)
        base_ref[slot + 1] = -0.5 * (minus - plus.T)
    for slot in range(5):
        acc_ref[slot] = jnp.zeros((size, size), F32)

    def one_unit(unit, carried):
        factors = [1.0] + [unit_ref[unit, k] for k in range(4)]
        held = total([base_ref[0]] + [factors[k] * base_ref[k] for k in range(1, 5)])
        squared = hermitian_square(held)
        shifted = squared - 0.75 * held
        result = hermitian_square(shifted) - 0.5625 * squared + 1.5 * held
        result = result * unit_ref[unit, 4]
        acc_ref[0] += result
        for k in range(1, 5):
            acc_ref[k] += factors[k] * result
        return carried

    lax.fori_loop(0, trip_count, one_unit, 0)
    real, imag = {}, {}
    held = acc_ref[0]
    real[0], imag[0] = 0.5 * (held + held.T), 0.5 * (held - held.T)
    for d in (1, 2):
        cos_held, sin_held = acc_ref[2 * d - 1], acc_ref[2 * d]
        cos_flip, sin_flip = cos_held.T, sin_held.T
        rc, jc = 0.5 * (cos_held + cos_flip), 0.5 * (cos_held - cos_flip)
        rs, js = 0.5 * (sin_held + sin_flip), 0.5 * (sin_held - sin_flip)
        real[d], imag[d] = rc - js, jc + rs
        real[-d], imag[-d] = rc + js, jc - rs
    spread = {d: (split(real[d]), split(imag[d]), split(real[d] + imag[d])) for d in range(-2, 3)}
    taken = [(split(vr_ref[b]), split(vi_ref[b]), split(vr_ref[b] + vi_ref[b])) for b in range(3)]
    for b in range(3):
        p, q, s = (total([mm3(taken[e][k], spread[b - e][k]) for e in range(3)]) for k in range(3))
        out_real = p - q
        even, odd = cos_row * out_real, sin_row * (s - p - q)
        out_ref[3 + b] = out_real
        out_ref[6 + b] = even - odd
        out_ref[b] = even + odd


def ortho_taps(row, units, taps):
    size = taps.shape[1]
    scratch = [pltpu.VMEM((count, size, size), F32) for count in (5, 5, 3, 3)]
    return pl.pallas_call(
        functools.partial(ortho_kernel, units.shape[0]),
        out_shape=jax.ShapeDtypeStruct(taps.shape, F32),
        in_specs=[pl.BlockSpec(memory_space=pltpu.SMEM)] * 2 + [pl.BlockSpec(memory_space=pltpu.VMEM)],
        out_specs=pl.BlockSpec(memory_space=pltpu.VMEM),
        scratch_shapes=scratch,
        compiler_params=pltpu.CompilerParams(vmem_limit_bytes=56 << 20),
    )(row, units, taps)


def unit_tables(side, devices, scale):
    half = side // 2
    per = -(-side * half // devices)
    assert half % per == 0
    turn = 2.0 * np.pi / side
    rows = np.zeros((devices, 2))
    units = np.zeros((devices, per + 1, 5))
    for device in range(devices):
        k1, first = divmod(device * per, half)
        if k1 >= side:
            continue
        mirror = k1 % half == 0
        rows[device] = np.cos(turn * k1), np.sin(turn * k1)
        chosen = []
        for j in range(first, first + per):
            if j == 0:
                chosen.append((0 if k1 <= half else half, 1.0 if mirror else 2.0))
            else:
                chosen.append((j, 2.0))
        chosen.append((half, 1.0 if mirror and first == 0 else 0.0))
        for slot, (k2, weight) in enumerate(chosen):
            angle = turn * k2
            units[device, slot] = (
                np.cos(angle),
                np.sin(angle),
                np.cos(2 * angle),
                np.sin(2 * angle),
                weight * scale / side**2,
            )
    return jnp.asarray(rows, F32), jnp.asarray(units, F32)


def gradient_terms(inputs, cotangent):
    channels = inputs.shape[3]
    flat_cotangent = cotangent.reshape(-1, channels)
    collected = []
    for tap_index in range(9):
        row_off = tap_index // 3 - 1
        col_off = tap_index % 3 - 1
        shifted = jnp.roll(inputs, (-row_off, -col_off), axis=(1, 2))
        collected.append(mm(shifted.reshape(-1, channels), flat_cotangent, (0, 0)))
    return jnp.stack(collected)


class Layout:
    def __init__(self, mesh):
        self.wide, self.narrow = mesh.shape["dp"], mesh.shape["inner"]
        assert self.wide & (self.wide - 1) == 0 and self.narrow & (self.narrow - 1) == 0
        self.low = min(2, self.wide)
        self.middle = min(2, self.wide // self.low)
        self.outer = self.wide // (self.low * self.middle)

    def send(self, value, wide_flip, narrow_flip):
        pairs = [
            (d * self.narrow + i, (d ^ wide_flip) * self.narrow + (i ^ narrow_flip))
            for d in range(self.wide)
            for i in range(self.narrow)
        ]
        return lax.ppermute(value, ("dp", "inner"), pairs)

    def plane(self):
        return [(m, i) for m in range(self.middle) for i in range(self.narrow)]

    def scatter_sum(self, pick):
        kept = pick(0)
        for c in range(1, self.low):
            arrived = self.send(pick(c), c, 0)
            kept = kept + arrived
        return kept


def body(layout, inputs, cotangent, kernel_taps):
    channels = inputs.shape[3]
    side = inputs.shape[1]
    wide, narrow = layout.wide, layout.narrow
    low, middle, outer = layout.low, layout.middle, layout.outer
    rows, cols = kernel_taps.shape[1], kernel_taps.shape[2]
    at_wide, at_narrow = lax.axis_index("dp"), lax.axis_index("inner")
    at_low = at_wide % low
    at_middle = at_wide // low % middle
    at_outer = at_wide // (low * middle)

    def gather(block):
        held = jnp.stack([block] + [layout.send(block, o * low * middle, 0) for o in range(1, outer)])
        held = jnp.stack(
            [held] + [layout.send(held, m * low, i) for m, i in layout.plane()[1:]]
        ).reshape(middle, narrow, *held.shape)
        return jnp.stack([held] + [layout.send(held, c, 0) for c in range(1, low)])

    def as_matrices(blocks):
        return blocks.transpose(4, 0, 1, 3, 5, 2, 6).reshape(9, channels, channels)

    def as_blocks(matrices):
        cut = matrices.reshape(9, low, middle, outer, rows, narrow, cols)
        return cut.transpose(1, 2, 5, 3, 0, 4, 6)

    taps_all = gather(kernel_taps)
    terms = gradient_terms(inputs, cotangent).reshape(9, outer, middle, low, rows, narrow, cols)

    def part(value, axis, index):
        return lax.dynamic_index_in_dim(value, index, axis, keepdims=False)

    held = part(terms, 3, at_low)
    for c in range(1, low):
        held = held + layout.send(part(terms, 3, at_low ^ c), c, 0)
    pick = lambda m, i: part(part(held, 2, at_middle ^ m), 3, at_narrow ^ i)
    arrived = [layout.send(pick(m, i), m * low, i) for m, i in layout.plane()[1:]]
    held_plane = total([pick(0, 0)] + arrived)
    arrived = [layout.send(part(held_plane, 1, at_outer ^ o), o * low * middle, 0) for o in range(1, outer)]
    gradient = total([part(held_plane, 1, at_outer)] + arrived)

    gradient_all = gather(gradient)
    norm = jnp.sqrt(jnp.sum(gradient_all * gradient_all))
    step_factor = step_share * math.sqrt(channels) / (norm + 1e-06)
    updated = as_matrices(taps_all - step_factor * gradient_all)

    row_table, unit_table = unit_tables(side, wide * narrow, math.sqrt(channels))
    linear = at_wide * narrow + at_narrow
    blocks = as_blocks(ortho_taps(row_table[linear], unit_table[linear], updated))

    held = blocks[0]
    for c in range(1, low):
        held = held + layout.send(blocks[c], c, 0)
    held = total([held[0, 0]] + [layout.send(held[m, i], m * low, i) for m, i in layout.plane()[1:]])
    return total([held[0]] + [layout.send(held[o], o * low * middle, 0) for o in range(1, outer)])


def solution(mesh):
    placed = (
        P(("dp", "inner"), None, None, None),
        P(("dp", "inner"), None, None, None),
        P(None, "dp", "inner"),
    )
    return jax.shard_map(
        functools.partial(body, Layout(mesh)),
        mesh=mesh,
        in_specs=placed,
        out_specs=P(None, "dp", "inner"),
        check_vma=False,
    )
```

```python
import functools
import math

import jax
import jax.numpy as jnp
import numpy as np
from jax import lax
from jax.experimental import pallas as pl
from jax.experimental.pallas import tpu as pltpu
from jax.sharding import PartitionSpec as P

F32 = jnp.float32
BF16 = jnp.bfloat16
VMEM_BYTES = 56 << 20
TAIL = 8

step_share = 0.06


def vmem_specs(count):
    return [pl.BlockSpec(memory_space=pltpu.VMEM)] * count


def smem_specs(count):
    return [pl.BlockSpec(memory_space=pltpu.SMEM)] * count


def vmem_call(kernel, outs, args, smem=0, scratch=(), cost=None):
    return pl.pallas_call(
        kernel,
        out_shape=outs,
        in_specs=smem_specs(smem) + vmem_specs(len(args) - smem),
        out_specs=jax.tree.map(lambda _: vmem_specs(1)[0], outs),
        scratch_shapes=list(scratch),
        compiler_params=pltpu.CompilerParams(vmem_limit_bytes=VMEM_BYTES),
        cost_estimate=cost,
    )(*args)


def shape_of(*dims, dtype=F32):
    return jax.ShapeDtypeStruct(dims, dtype)


def total(terms):
    return functools.reduce(lambda a, b: a + b, terms)


def split(value):
    high = value.astype(BF16)
    return high, (value - high.astype(F32)).astype(BF16)


def mm(left, right, contract=(1, 0)):
    dims = (((contract[0],), (contract[1],)), ((), ()))
    return lax.dot_general(left, right, dims, preferred_element_type=F32)


def mm3(left, right, contract=(1, 0)):
    (lh, ll), (rh, rl) = left, right
    return mm(lh, rh, contract) + (mm(lh, rl, contract) + mm(ll, rh, contract))


def hermitian_square(held):
    skew = 0.5 * (held - held.T)
    held_parts, skew_parts = split(held), split(skew)
    return mm3(held_parts, held_parts) - 2.0 * mm3(skew_parts, skew_parts)


def ortho_kernel(size, places, stacked, summed, unit_count, own_ref, unit_ref, *refs):
    count = len(places)
    ins, outs = refs[: (1 + summed) * count], refs[(1 + summed) * count : -4]
    taps_refs, grad_refs = ins[:count], ins[count:]
    base_ref, acc_ref, vr_ref, vi_ref = refs[-4:]
    even_mix, odd_mix = own_ref[0], own_ref[1]
    if summed:
        square_sum = total([g[-TAIL:][:1] for g in grad_refs])
        factor = step_share * math.sqrt(size) / (jnp.sqrt(square_sum) + 1e-06)
    for index, (row, column, height, width) in enumerate(places):
        for b in range(3):
            lo, hi = b * height, (b + 3) * height
            first, second = taps_refs[index][lo : lo + height], taps_refs[index][hi : hi + height]
            if summed:
                first = first - factor * grad_refs[index][lo : lo + height]
                second = second - factor * grad_refs[index][hi : hi + height]
            vr_ref[b, row : row + height, column : column + width] = first + even_mix * second
            vi_ref[b, row : row + height, column : column + width] = odd_mix * second
    diag = lax.broadcasted_iota(jnp.int32, (size, size), 0) == lax.broadcasted_iota(jnp.int32, (size, size), 1)
    own = []
    for b in range(3):
        x, y = vr_ref[b], vi_ref[b]
        y_parts = split(y)
        own.append(mm3(split(x - y), split(x + y), (0, 0)) + 2.0 * mm3(y_parts, y_parts, (0, 0)))
    base_ref[0] = jnp.where(diag, 1.5, 0.0) - 0.5 * total(own)
    for slot, pairs in ((1, ((1, 0), (2, 1))), (3, ((2, 0),))):
        plus, minus = [], []
        for left, right in pairs:
            ar, ai = split(vr_ref[left]), split(vi_ref[left])
            add = split(vr_ref[right] + vi_ref[right])
            sub = split(vr_ref[right] - vi_ref[right])
            plus.append(mm3(ar, add, (0, 0)) - mm3(ai, sub, (0, 0)))
            minus.append(mm3(ar, sub, (0, 0)) + mm3(ai, add, (0, 0)))
        plus, minus = total(plus), total(minus)
        base_ref[slot] = -0.5 * (plus + minus.T)
        base_ref[slot + 1] = -0.5 * (minus - plus.T)
    for slot in range(5):
        acc_ref[slot] = jnp.zeros((size, size), F32)

    def one_unit(unit, carried):
        factors = [1.0] + [unit_ref[unit, k] for k in range(4)]
        held = total([base_ref[0]] + [factors[k] * base_ref[k] for k in range(1, 5)])
        squared = hermitian_square(held)
        shifted = squared - 0.75 * held
        result = hermitian_square(shifted) - 0.5625 * squared + 1.5 * held
        result = result * unit_ref[unit, 4]
        acc_ref[0] += result
        for k in range(1, 5):
            acc_ref[k] += factors[k] * result
        return carried

    lax.fori_loop(0, unit_count, one_unit, 0)

    @pl.when(unit_ref[unit_count, 4] != 0.0)
    def _():
        one_unit(unit_count, 0)

    real, imag = {}, {}
    held = acc_ref[0]
    real[0], imag[0] = 0.5 * (held + held.T), 0.5 * (held - held.T)
    for d in (1, 2):
        cos_held, sin_held = acc_ref[2 * d - 1], acc_ref[2 * d]
        cos_flip, sin_flip = cos_held.T, sin_held.T
        rc, jc = 0.5 * (cos_held + cos_flip), 0.5 * (cos_held - cos_flip)
        rs, js = 0.5 * (sin_held + sin_flip), 0.5 * (sin_held - sin_flip)
        real[d], imag[d] = rc - js, jc + rs
        real[-d], imag[-d] = rc + js, jc - rs
    spread = {d: (split(real[d]), split(imag[d]), split(real[d] + imag[d])) for d in range(-2, 3)}
    taken = [(split(vr_ref[b]), split(vi_ref[b]), split(vr_ref[b] + vi_ref[b])) for b in range(3)]
    for b in range(3):
        p, q, s = (total([mm3(taken[e][k], spread[b - e][k]) for e in range(3)]) for k in range(3))
        first = p - q
        second = even_mix * first - odd_mix * (s - p - q)
        for index, (row, column, height, width) in enumerate(places):
            last = index - (count - stacked)
            out = outs[index] if last < 0 else outs[count - stacked].at[last]
            lo, hi = b * height, (b + 3) * height
            out[lo : lo + height] = first[row : row + height, column : column + width]
            out[hi : hi + height] = second[row : row + height, column : column + width]


def ortho_pieces(size, places, stacked, own, units, taps, grads):
    count = units.shape[0] - 1
    outs = [shape_of(6 * h, w) for _, _, h, w in places[: len(places) - stacked]]
    if stacked:
        outs.append(shape_of(stacked, 6 * places[-1][2], places[-1][3]))
    return vmem_call(
        functools.partial(ortho_kernel, size, places, stacked, bool(grads), count),
        outs,
        [own, units, *taps, *grads],
        smem=2,
        scratch=[pltpu.VMEM((k, size, size), F32) for k in (5, 5, 3, 3)],
        cost=pl.CostEstimate(flops=2 * 3 * (50 + 4 * count) * size**3, bytes_accessed=1, transcendentals=0),
    )


def gradient_kernel(samples, side, store, place_ref, inputs_ref, cotangent_ref, *refs):
    *outs, turned_ref, padded_ref = refs
    area = side * side
    for sample in range(samples):
        turned_ref[...] = inputs_ref[sample].T
        value = cotangent_ref[sample].astype(F32)
        column = lax.broadcasted_iota(jnp.int32, value.shape, 0) % side
        down, up = jnp.roll(value, 1, 0), jnp.roll(value, -1, 0)
        back = jnp.where(column == 0, jnp.roll(down, -side, 0), down)
        ahead = jnp.where(column == side - 1, jnp.roll(up, side, 0), up)
        for b, moved in enumerate((ahead, value, back)):
            moved = moved.astype(BF16)
            padded_ref[b, side : side + area] = moved
            padded_ref[b, :side] = moved[area - side :]
            padded_ref[b, side + area :] = moved[:side]
        for tap in range(9):
            start = (2 - tap // 3) * side
            product = mm(turned_ref[...], padded_ref[tap % 3, start : start + area])
            store(place_ref, outs, sample, tap, product)


def gradient_call(store, out, place, inputs, cotangent):
    samples, side, _, channels = inputs.shape
    area = side * side
    return vmem_call(
        functools.partial(gradient_kernel, samples, side, store),
        [out],
        [place, inputs.reshape(samples, area, channels), cotangent.reshape(samples, area, channels)],
        smem=1,
        scratch=[pltpu.VMEM((channels, area), BF16), pltpu.VMEM((3, area + 2 * side, channels), BF16)],
        cost=pl.CostEstimate(flops=18 * samples * area * channels**2, bytes_accessed=1, transcendentals=0),
    )[0]


def unit_tables(side, devices, scale):
    half = side // 2
    per = -(-side * half // devices)
    assert devices % 2 == 0 and half % per == 0
    parts = half // per
    turn = 2.0 * np.pi / side
    mixes = np.zeros((devices // 2, 3))
    own = np.zeros((devices, 2))
    units = np.zeros((devices, per + 1, 5))
    for device in range(devices):
        pair, core = divmod(device, 2)
        k1, part = divmod(pair, parts)
        if k1 >= half:
            continue
        mirror = k1 == 0
        mixes[pair] = (0.0, 1.0, 0.0) if mirror else (np.cos(turn * k1), 0.0, np.sin(turn * k1))
        sign = 1.0 if core == 0 else -1.0
        own[device] = (sign, 0.0) if mirror else (0.0, -sign)
        edge = 0 if core == 0 or mirror else half
        chosen = []
        for j in range(part * per, (part + 1) * per):
            chosen.append((j, 2.0) if j else (edge, 1.0 if mirror else 2.0))
        chosen.append((half, 1.0 if mirror and part == 0 else 0.0))
        for slot, (k2, weight) in enumerate(chosen):
            angle = turn * k2
            trig = np.cos(angle), np.sin(angle), np.cos(2 * angle), np.sin(2 * angle)
            units[device, slot] = *trig, weight * scale / side**2
    return mixes, own, units


def glue_call(steps, outs, mix, arrays):
    def kernel(mix_ref, *refs):
        ins, results = refs[: len(arrays)], refs[len(arrays) :]
        for out, start, value in steps(lambda t, k: mix_ref[t, k], ins):
            results[out][start : start + value.shape[0]] = value

    return vmem_call(kernel, [shape_of(*o) for o in outs], [mix, *arrays], smem=1)


def spread_steps(rows, tail, targets, mix, blocks):
    count = len(blocks)
    for o, block in enumerate(blocks):
        for b in range(3):
            low, mid, top = (block[(3 * a + b) * rows : (3 * a + b + 1) * rows] for a in range(3))
            even, odd = top + low, top - low
            for t in range(targets):
                yield t, (b * count + o) * rows, mid + mix(t, 0) * even
                yield t, ((b + 3) * count + o) * rows, mix(t, 1) * even + mix(t, 2) * odd
    if tail:
        sums = total([block[9 * rows : 9 * rows + TAIL] for block in blocks])
        for t in range(targets):
            yield t, 6 * count * rows, sums


def expand_steps(rows, count, mix, pieces):
    for o in range(count):
        for b in range(3):
            mids, tops, lows = [], [], []
            for t, piece in enumerate(pieces):
                lo, hi = (b * count + o) * rows, ((b + 3) * count + o) * rows
                first, second = piece[lo : lo + rows], piece[hi : hi + rows]
                even, odd = mix(t, 0) * first + mix(t, 1) * second, mix(t, 2) * second
                mids.append(first)
                tops.append(even - odd)
                lows.append(even + odd)
            for a, terms in enumerate((lows, mids, tops)):
                yield o, (3 * a + b) * rows, total(terms)


def body(wide, narrow, inputs, cotangent, kernel_taps):
    samples, side, _, channels = inputs.shape
    rows, cols = kernel_taps.shape[1], kernel_taps.shape[2]
    low = 2
    middle = min(2, wide // low)
    outer = wide // (low * middle)
    height = outer * rows
    plane = [(m, i) for m in range(middle) for i in range(narrow)]

    at_wide, at_narrow = lax.axis_index("dp"), lax.axis_index("inner")
    at_middle, at_outer, at_low = at_wide // low % middle, at_wide // (low * middle), at_wide % low
    at_pair = at_wide // low * narrow + at_narrow

    def send(value, outer_flip=0, middle_flip=0, low_flip=0, narrow_flip=0):
        flip = (outer_flip * middle + middle_flip) * low + low_flip
        pairs = [
            (d * narrow + i, (d ^ flip) * narrow + (i ^ narrow_flip)) for d in range(wide) for i in range(narrow)
        ]
        return lax.ppermute(value, ("dp", "inner"), pairs)

    mixes, own_table, unit_table = unit_tables(side, wide * narrow, math.sqrt(channels))
    partners = jnp.stack([at_wide // low ^ m for m, _ in plane]) * narrow + jnp.stack([at_narrow ^ i for _, i in plane])
    mix = jnp.asarray(mixes, F32)[partners]
    own = jnp.asarray(own_table, F32)[at_pair * low + at_low]
    units = jnp.asarray(unit_table, F32)[at_pair * low + at_low]

    place = jnp.stack([at_outer, at_middle, at_low, at_narrow]).astype(jnp.int32)
    if rows % 16 or cols % 128:
        return plain_body(place, mix[:1], own, units, inputs, cotangent, kernel_taps)

    def store(place_ref, outs, sample, tap, product):
        for index in range(wide * narrow):
            upper, i = divmod(index, narrow)
            o, m, c = upper // (low * middle), upper // low % middle, upper % low
            block = product[upper * rows : (upper + 1) * rows, i * cols : (i + 1) * cols]
            slot = (m ^ place_ref[1]) * narrow + (i ^ place_ref[3])
            at = outs[0].at[c ^ place_ref[2], slot, o ^ place_ref[0], tap]
            at[...] = block if sample == 0 else at[...] + block

    terms = shape_of(low, len(plane), outer, 9, rows, cols)
    terms = gradient_call(store, terms, place, inputs, cotangent)
    kept, sent = terms.reshape(low, len(plane), outer * 9 * rows, cols)
    arrived = send(sent, low_flip=1)
    kernel_taps, kept, arrived = lax.optimization_barrier((kernel_taps, kept, arrived))
    own_taps = kernel_taps.reshape(9 * rows, cols)
    taps_outer = [own_taps] + [send(own_taps, outer_flip=o) for o in range(1, outer)]
    held = [kept[p] + arrived[p] for p in range(len(plane))]
    got = [send(held[p], middle_flip=m, narrow_flip=i) for p, (m, i) in enumerate(plane) if p]
    held = total([held[0]] + got)
    held = [held[9 * rows * o : 9 * rows * (o + 1)] for o in range(outer)]

    shapes = [(6 * height, cols)] * len(plane)
    taps_spread = glue_call(functools.partial(spread_steps, rows, False, len(plane)), shapes, mix, taps_outer)
    held, taps_spread = lax.optimization_barrier((held, taps_spread))

    def gather_pieces(spread):
        near = [spread[0]] + [send(spread[p], middle_flip=m, narrow_flip=i) for p, (m, i) in enumerate(plane) if p]
        return near + [send(piece, low_flip=1) for piece in near]

    taps_pieces = gather_pieces(taps_spread)
    got = [send(held[o], outer_flip=o) for o in range(1, outer)]
    gradient = total([held[0]] + got)
    gradient, taps_pieces = lax.optimization_barrier((gradient, taps_pieces))

    square_sum = jnp.sum(gradient * gradient)
    payload = jnp.concatenate([gradient, jnp.full((TAIL, cols), square_sum)])
    grad_outer = [payload] + [send(payload, outer_flip=o) for o in range(1, outer)]
    shapes = [(6 * height + TAIL, cols)] * len(plane)
    grad_spread = glue_call(functools.partial(spread_steps, rows, True, len(plane)), shapes, mix, grad_outer)
    grad_pieces = gather_pieces(grad_spread)

    places = [((c * middle + m) * height, i * cols, height, cols) for c in range(low) for m, i in plane]
    *kept, sent = ortho_pieces(channels, places, len(plane), own, units, taps_pieces, grad_pieces)

    arrived = send(sent, low_flip=1)
    held = [kept[p] + arrived[p] for p in range(len(plane))]
    got = [held[0]] + [send(held[p], middle_flip=m, narrow_flip=i) for p, (m, i) in enumerate(plane) if p]
    held = glue_call(functools.partial(expand_steps, rows, outer), [(9 * rows, cols)] * outer, mix, got)
    result = total([held[0]] + [send(held[o], outer_flip=o) for o in range(1, outer)])
    return result.reshape(9, rows, cols)


def plain_body(place, mix, own, units, inputs, cotangent, kernel_taps):
    channels = inputs.shape[3]

    def store(place_ref, outs, sample, tap, product):
        outs[0][tap] = product if sample == 0 else outs[0][tap] + product

    def scatter(terms):
        terms = lax.psum_scatter(terms, "dp", scatter_dimension=1, tiled=True)
        return lax.psum_scatter(terms, "inner", scatter_dimension=2, tiled=True)

    gradient = scatter(gradient_call(store, shape_of(9, channels, channels), place, inputs, cotangent))
    square_sum = lax.psum(jnp.sum(gradient * gradient), ("dp", "inner"))
    updated = kernel_taps - step_share * math.sqrt(channels) / (jnp.sqrt(square_sum) + 1e-06) * gradient
    updated = lax.all_gather(updated, "inner", axis=2, tiled=True)
    updated = lax.all_gather(updated, "dp", axis=1, tiled=True).reshape(9 * channels, channels)
    factors = lambda t, k: mix[t, k]
    pieces = [value for _, _, value in sorted(spread_steps(channels, False, 1, factors, [updated]), key=lambda e: e[1])]
    places = [(0, 0, channels, channels)]
    pieces = ortho_pieces(channels, places, 0, own, units, [jnp.concatenate(pieces)], [])
    taps = [value for _, _, value in sorted(expand_steps(channels, 1, factors, pieces), key=lambda e: e[1])]
    return scatter(jnp.stack(taps))


def solution(mesh):
    wide, narrow = mesh.shape["dp"], mesh.shape["inner"]
    assert wide & (wide - 1) == 0 and narrow & (narrow - 1) == 0 and wide % 2 == 0
    placed = (
        P(("dp", "inner"), None, None, None),
        P(("dp", "inner"), None, None, None),
        P(None, "dp", "inner"),
    )
    return jax.shard_map(
        functools.partial(body, wide, narrow),
        mesh=mesh,
        in_specs=placed,
        out_specs=P(None, "dp", "inner"),
        check_vma=False,
    )
```
